32 devices in a mesh: pipe: 16 (over z, y, core), tensor: 2 (over x).
Axes of the slice: x: 2, y: 2, z: 4, core: 2. Of those that a mesh axis runs over, the one named last changes fastest.
Arguments:
- tokens_x: bfloat16 [16, 384, 12288], P('pipe', None, 'tensor'), may hold values from -6 to 6
- queries: bfloat16 [16, 384, 12288], P('pipe', None, 'tensor'), may hold values from -120 to 120
- key_rows: bfloat16 [16, 384, 1024], P('pipe', None, 'tensor'), may hold values from -5 to 5
- out_grad: bfloat16 [16, 384, 12288], P('pipe', None, 'tensor'), may hold values from -4 to 4
- value_weight: bfloat16 [16, 12288, 1024], P('pipe', 'tensor'), may hold values from -0.0546875 to 0.0546875
- doc_starts: int32 [16, 384], P('pipe'), may hold values from 0 to 383, as said below
Outputs:
- query_grad: bfloat16 [16, 384, 12288], P('pipe', None, 'tensor')
- key_grad: bfloat16 [16, 384, 1024], P('pipe', None, 'tensor')
- weight_grad: bfloat16 [16, 12288, 1024], P('pipe', 'tensor')
- section_grad: bfloat16 [16, 384, 12288], P('pipe', None, 'tensor')
The draws below stay inside these ranges and needn't reach their ends.
Inputs may be any that keep to these rules, and one draw needn't show every extreme that they name: doc_starts[s, 0] = 0, doc_starts[s, 383] = 383, doc_starts[s, i] <= i, and doc_starts[s, i] is either doc_starts[s, i - 1] or i.
All inputs are finite; a program needn't handle non-finite values.
Results may differ from the reference program's by a relative error of at most 0.012.
The reference program's roundings to bfloat16 on the way count: a program that leaves them out, or rounds other values in their place, can miss the bound.
Values may be sent and summed in bfloat16 or wider, within the bound.
A program may use at most 256 MiB of HBM per device.

```python
import jax
import jax.numpy as jnp
from jax import lax

D = 12288
HQ = 96
KV = 8
HD = 128
TOK = 384
SECTIONS = 16


def paired_draw(key):
    base = jax.random.fold_in(key, 101)
    key_k, key_q = jax.random.split(base, 2)
    keys_all = jnp.clip(jax.random.normal(key_k, (SECTIONS, TOK, KV, HD), jnp.float32), -5.0, 5.0)
    queries_all = jnp.clip(jax.random.normal(key_q, (SECTIONS, TOK, KV, HQ // KV, HD), jnp.float32), -5.0, 5.0)
    return (queries_all.reshape(SECTIONS, TOK, HQ * HD), keys_all.reshape(SECTIONS, TOK, KV * HD))


def draw_queries(key, part):
    return paired_draw(key)[0].astype(jnp.bfloat16)


def draw_key_rows(key, part):
    return paired_draw(key)[1].astype(jnp.bfloat16)


def draw_doc_starts(key, part):
    flags = jax.random.randint(jax.random.fold_in(key, 202), (SECTIONS, TOK), 0, 48) == 0
    position = jnp.arange(TOK, dtype=jnp.int32)[None, :]
    marked = jnp.where(flags | (position == 0) | (position == TOK - 1), position, 0).astype(jnp.int32)
    return lax.cummax(marked, axis=1).astype(jnp.int32)


def steps_of(rng, extent, cuts, least, high):
    gain = 1.0
    for axis_at, parts in cuts:
        steps = jax.random.uniform(jax.random.fold_in(jax.random.fold_in(rng, 6), axis_at), (parts,), jnp.float32, least / len(cuts), high / len(cuts))
        gain = gain * jnp.repeat(jnp.exp(steps), extent[axis_at] // parts).reshape((-1,) + (1,) * (len(extent) - 1 - axis_at))
    return gain


def normal_values(key, shape, width, bound, cuts=(), held_as=jnp.bfloat16):
    drawn = width * jax.random.normal(key, shape, jnp.float32)
    if cuts:
        drawn = drawn * steps_of(key, shape, cuts, -0.22, 0.18)
    return jnp.clip(drawn, -bound, bound).astype(held_as)


def setup_inputs(seed: int = 0) -> dict:
    key_of = jax.random.split(jax.random.key(seed), 7)
    tokens_x = normal_values(key_of[0], (SECTIONS, TOK, D), 1.0, 6.0, ((0, 16), (2, 2)))
    queries = draw_queries(jax.random.fold_in(key_of[6], 71), 0)
    key_rows = draw_key_rows(jax.random.fold_in(key_of[6], 71), 0)
    out_grad = normal_values(key_of[3], (SECTIONS, TOK, HQ * HD), 0.25, 4.0, ((0, 16), (2, 2)))
    value_weight = normal_values(key_of[4], (SECTIONS, D, KV * HD), D ** -0.5, 0.0546875, ((0, 16), (1, 2)))
    doc_starts = draw_doc_starts(jax.random.fold_in(key_of[6], 71), 0)
    return dict(tokens_x=tokens_x, queries=queries, key_rows=key_rows, out_grad=out_grad, value_weight=value_weight, doc_starts=doc_starts)


def attend(queries, key_rows, values, out_grad, doc_starts):
    length = queries.shape[0]
    kv_heads = key_rows.shape[1] // HD
    groups = queries.shape[1] // (kv_heads * HD)
    scaling = HD ** -0.5
    row_index = lax.broadcasted_iota(jnp.int32, (length, length), 0)
    col_index = lax.broadcasted_iota(jnp.int32, (length, length), 1)
    allowed = (col_index <= row_index) & (col_index >= doc_starts[:, None])
    query_heads = queries.reshape(length, kv_heads, groups, HD)
    key_heads = key_rows.reshape(length, kv_heads, HD)
    value_heads = values.reshape(length, kv_heads, HD)
    grad_heads = out_grad.reshape(length, kv_heads, groups, HD)

    def one_group(query_g, key_g, value_g, grad_g):
        query_f = query_g.astype(jnp.float32)
        key_f = key_g.astype(jnp.float32)
        value_f = value_g.astype(jnp.float32)
        grad_f = grad_g.astype(jnp.float32)
        scores = jnp.einsum("igd,jd->gij", query_f, key_f) * scaling
        scores = jnp.where(allowed[None], scores, -1e30)
        top_score = jnp.max(scores, axis=2, keepdims=True)
        expo = jnp.exp(scores - top_score)
        probs = expo / jnp.sum(expo, axis=2, keepdims=True)
        probs_low = lax.optimization_barrier(probs.astype(jnp.bfloat16)).astype(jnp.float32)
        attended = jnp.einsum("gij,jd->igd", probs_low, value_f)
        delta = jnp.sum(grad_f * attended, axis=2)
        grad_probs = jnp.einsum("igd,jd->gij", grad_f, value_f)
        grad_scores = probs * (grad_probs - delta.T[:, :, None])
        scaled_low = lax.optimization_barrier((grad_scores * scaling).astype(jnp.bfloat16)).astype(jnp.float32)
        grad_query = jnp.einsum("gij,jd->igd", scaled_low, key_f).astype(jnp.bfloat16)
        grad_key = jnp.einsum("gij,igd->jd", scaled_low, query_f).astype(jnp.bfloat16)
        grad_value = jnp.einsum("gij,igd->jd", probs_low, grad_f).astype(jnp.bfloat16)
        return grad_query, grad_key, grad_value

    grad_query, grad_key, grad_value = jax.vmap(one_group, in_axes=(1, 1, 1, 1), out_axes=(1, 1, 1))(
        query_heads, key_heads, value_heads, grad_heads)
    return grad_query.reshape(length, -1), grad_key.reshape(length, -1), grad_value.reshape(length, -1)


def reference(tokens_x, queries, key_rows, out_grad, value_weight, doc_starts):
    def one_section(pieces):
        inputs, query_s, key_s, grad_s, weight_s, starts_s = pieces
        values = jnp.dot(inputs, weight_s, preferred_element_type=jnp.float32).astype(jnp.bfloat16)
        grad_query, grad_key, grad_value = attend(query_s, key_s, values, grad_s, starts_s)
        weight_grad = jnp.dot(inputs.T, grad_value, preferred_element_type=jnp.float32).astype(jnp.bfloat16)
        input_grad = jnp.dot(grad_value, weight_s.T, preferred_element_type=jnp.float32).astype(jnp.bfloat16)
        return grad_query, grad_key, weight_grad, input_grad

    query_grad, key_grad, weight_grad, input_grad = lax.map(
        one_section, (tokens_x, queries, key_rows, out_grad, value_weight, doc_starts))
    section_grad = jnp.concatenate([input_grad[1:], jnp.zeros_like(input_grad[:1])], axis=0)
    return (query_grad, key_grad, weight_grad, section_grad)
```

```python
import functools
import math

import jax
import jax.numpy as jnp
from jax import lax
from jax.experimental import pallas as pl
from jax.experimental.pallas import tpu as pltpu
from jax.sharding import PartitionSpec as P

HD = 128
BLOCKS = 4
SENT = 2
SCALING = HD ** (-0.5)
TO_EXP2 = SCALING * math.log2(math.e)
LOW = jnp.bfloat16
WIDE = jnp.float32
MESH = pl.DeviceIdType.MESH


def times(left, right, dims=((1,), (0,))):
    return lax.dot_general(left, right, (dims, ((), ())), preferred_element_type=WIDE)


def stacked(ref, rows, head, count):
    columns = pl.ds(pl.multiple_of(head * HD, HD), count * HD)
    block = ref[rows, columns]
    return jnp.concatenate([block[:, at * HD : (at + 1) * HD] for at in range(count)], axis=0)


def heads_together(rows, groups):
    for count in (2, 3, 4, 6, 8, 12):
        if groups % count == 0 and count * rows % HD == 0 and count * rows >= 256:
            return count
    return groups


def early_kernel(
    pipes,
    ranks,
    groups,
    tile,
    starts_hbm,
    query_hbm,
    grad_hbm,
    key_hbm,
    panel_hbm,
    inputs_hbm,
    came_ref,
    rest_ref,
    grad_all_ref,
    values_ref,
    *others,
):
    probs_out, others = others[:BLOCKS], others[BLOCKS:]
    bias, others = others[:BLOCKS], others[BLOCKS:]
    probs, others = others[:BLOCKS], others[BLOCKS:]
    own, others = others[:BLOCKS], others[BLOCKS:]
    came, others = others[:BLOCKS], others[BLOCKS:]
    (
        starts, query, grad, key, panel, inputs, total, grad_all, stage, zeros,
        part_own, part_send, part_came, values,
        in_sem, panel_sem, out_sem, grad_send, grad_recv, part_sent, part_recv,
        stage_send, stage_recv,
    ) = others
    length, width = query.shape
    slim = key.shape[1]
    kv_heads = slim // HD
    rows = length // BLOCKS
    together = heads_together(rows, groups)
    lanes = together * rows
    tiles = width // tile
    kept = length - SENT * rows
    me_p = lax.axis_index("pipe")
    me_t = lax.axis_index("tensor")

    def block_rows(at):
        return slice(at * rows, (at + 1) * rows)

    barrier = pltpu.get_barrier_semaphore()
    for step in range(1, ranks):
        peer = lax.rem(me_t + step, ranks)
        pl.semaphore_signal(barrier, inc=1, device_id=(me_p, peer), device_id_type=MESH)

    @pl.when(me_p > 0)
    def _():
        pl.semaphore_signal(barrier, inc=1, device_id=(me_p - 1, me_t), device_id_type=MESH)

    @pl.when(me_p < pipes - 1)
    def _():
        pl.semaphore_signal(barrier, inc=1, device_id=(me_p + 1, me_t), device_id_type=MESH)

    def load(source, target, sem):
        return pltpu.make_async_copy(source, target, in_sem.at[sem])

    def load_rows(source, target, at, sem):
        return load(source.at[block_rows(at)], target.at[block_rows(at)], sem + at)

    def load_panel(at):
        part = pl.ds(pl.multiple_of(at * tile, tile), tile)
        return pltpu.make_async_copy(panel_hbm.at[part], panel.at[part], panel_sem.at[at])

    last = BLOCKS - 1
    load(starts_hbm, starts, 0).start()
    load(key_hbm, key, 1).start()
    load_rows(query_hbm, query, last, 3).start()
    load_rows(grad_hbm, grad, last, 3 + BLOCKS).start()
    load(starts_hbm, starts, 0).wait()

    def fill_bias(at):
        shape = bias[at].shape
        token_j = lax.broadcasted_iota(jnp.int32, shape, 0)
        token_i = lax.broadcasted_iota(jnp.int32, (1, rows), 1) + at * rows
        first = starts[:, block_rows(at)]
        token_i = jnp.concatenate([token_i] * together, axis=1)
        first = jnp.concatenate([first] * together, axis=1)
        bias[at][...] = jnp.where((token_j <= token_i) & (token_j >= first), 0.0, -1e30)

    fill_bias(last)
    load(key_hbm, key, 1).wait()
    load_rows(query_hbm, query, last, 3).wait()
    load_rows(grad_hbm, grad, last, 3 + BLOCKS).wait()
    for at in range(tiles):
        load_panel(at).start()
    for at in range(last - 1, -1, -1):
        load_rows(query_hbm, query, at, 3).start()
        load_rows(grad_hbm, grad, at, 3 + BLOCKS).start()
    load(inputs_hbm, inputs, 2).start()

    def softmax(at, head):
        reach = (at + 1) * rows
        column = pl.ds(pl.multiple_of(head * HD, HD), HD)
        key_h = key[:reach, column]
        for part in range(groups // together):
            query_h = stacked(query, block_rows(at), head * groups + part * together, together)
            power = times(key_h, query_h, ((1,), (1,))) * TO_EXP2 + bias[at][...]
            top = jnp.max(power, axis=0, keepdims=True)
            expo = jnp.exp2(power - top)
            inverse = 1.0 / jnp.sum(expo, axis=0, keepdims=True)
            probs[at][head, :, part * lanes : (part + 1) * lanes] = (expo * inverse).astype(LOW)
        grad_h = stacked(grad, block_rows(at), head * groups, groups)
        term = times(probs[at][head], grad_h)
        if at == last:
            total[:reach, column] = term
        else:
            total[:reach, column] += term

    def softmax_heads(at, first, end):
        @pl.loop(first, end)
        def _(head):
            softmax(at, head)

    def grad_copy(at, step):
        peer = lax.rem(me_t + step, ranks)
        return pltpu.make_async_remote_copy(
            src_ref=own[at],
            dst_ref=came[at].at[step - 1],
            send_sem=grad_send.at[at, step - 1],
            recv_sem=grad_recv.at[at, step - 1],
            device_id=(me_p, peer),
            device_id_type=MESH,
        )

    def rank_columns(rank):
        return pl.ds(pl.multiple_of(rank * slim, HD), slim)

    def give(at):
        ready = total[block_rows(at), :].astype(LOW)
        own[at][...] = ready
        for step in range(1, ranks):
            grad_copy(at, step).start()
        grad_all[block_rows(at), rank_columns(me_t)] = ready
        pltpu.make_async_copy(probs[at], probs_out[at], out_sem.at[at]).start()

    def take(at):
        for step in range(1, ranks):
            grad_copy(at, step).wait_recv()
            rank = lax.rem(me_t + ranks - step, ranks)
            grad_all[block_rows(at), rank_columns(rank)] = came[at][step - 1]

    def stage_copy(slot, at):
        part = pl.ds(pl.multiple_of(at * tile, tile), tile)
        first = length - (slot + 1) * rows
        return pltpu.make_async_remote_copy(
            src_ref=stage.at[first : first + rows, part],
            dst_ref=came_ref.at[first - kept : first - kept + rows, part],
            send_sem=stage_send.at[slot, at],
            recv_sem=stage_recv.at[slot, at],
            device_id=(me_p - 1, me_t),
            device_id_type=MESH,
        )

    def input_grad(first, end, slots, panel_wait):
        @pl.loop(0, tiles)
        def _(at):
            if panel_wait:
                load_panel(at).wait()
            part = pl.ds(pl.multiple_of(at * tile, tile), tile)
            result = times(grad_all[first:end, :], panel[part, :], ((1,), (1,)))
            stage[first:end, part] = result.astype(LOW)

            @pl.when(me_p > 0)
            def _():
                for slot in slots:
                    stage_copy(slot, at).start()

    def wait_rows(at):
        load_rows(query_hbm, query, at, 3).wait()
        load_rows(grad_hbm, grad, at, 3 + BLOCKS).wait()

    def part_values(rank, target):
        column = 256 if slim % 256 == 0 else HD
        for at in range(0, slim, column):
            part = pl.ds(pl.multiple_of(rank * slim + at, HD), column)
            target[:, at : at + column] = times(inputs[...], panel[:, part]).astype(target.dtype)

    def part_copy(step):
        peer = lax.rem(me_t + step, ranks)
        return pltpu.make_async_remote_copy(
            src_ref=part_send.at[step - 1],
            dst_ref=part_came.at[step - 1],
            send_sem=part_sent.at[step - 1],
            recv_sem=part_recv.at[step - 1],
            device_id=(me_p, peer),
            device_id_type=MESH,
        )

    softmax_heads(last, 0, kv_heads)
    greeted = ranks - 1 + lax.min(me_p, 1) + lax.min(pipes - 1 - me_p, 1)
    pl.semaphore_wait(barrier, greeted)

    give(last)
    early = kv_heads // 2
    fill_bias(last - 1)
    wait_rows(last - 1)
    if early:
        softmax_heads(last - 1, 0, early)
    take(last)
    input_grad(length - rows, length, (0,), True)
    softmax_heads(last - 1, early, kv_heads)
    give(last - 1)
    for at in range(last - 2, -1, -1):
        fill_bias(at)
        wait_rows(at)
        softmax_heads(at, 0, kv_heads)
        give(at)
    load(inputs_hbm, inputs, 2).wait()
    for step in range(1, ranks):
        part_values(lax.rem(me_t + step, ranks), part_send.at[step - 1])
        part_copy(step).start()
    for at in range(last - 1, -1, -1):
        take(at)
    input_grad(0, length - rows, tuple(range(1, SENT)), False)
    rest_copy = pltpu.make_async_copy(stage.at[:kept], rest_ref, out_sem.at[BLOCKS])
    rest_copy.start()
    all_copy = pltpu.make_async_copy(grad_all, grad_all_ref, out_sem.at[BLOCKS + 1])
    all_copy.start()
    part_values(me_t, part_own)
    sum_all = part_own[...]
    for step in range(1, ranks):
        part_copy(step).wait_recv()
        sum_all = sum_all + part_came[step - 1].astype(WIDE)
    values[...] = sum_all.astype(LOW)
    values_copy = pltpu.make_async_copy(values, values_ref, out_sem.at[BLOCKS + 2])
    values_copy.start()

    @pl.when(me_p == pipes - 1)
    def _():
        zeros[...] = jnp.zeros_like(zeros)
        for slot in range(SENT):
            for at in range(tiles):
                part = slice(at * tile, (at + 1) * tile)
                copy = pltpu.make_async_copy(
                    zeros, came_ref.at[slot * rows : (slot + 1) * rows, part], out_sem.at[BLOCKS + 3]
                )
                copy.start()
                copy.wait()

    rest_copy.wait()
    all_copy.wait()
    values_copy.wait()
    for at in range(BLOCKS):
        pltpu.make_async_copy(probs[at], probs_out[at], out_sem.at[at]).wait()
        for step in range(1, ranks):
            grad_copy(at, step).wait_send()
    for step in range(1, ranks):
        part_copy(step).wait_send()

    @pl.when(me_p > 0)
    def _():
        for slot in range(SENT):
            for at in range(tiles):
                stage_copy(slot, at).wait_send()

    @pl.when(me_p < pipes - 1)
    def _():
        for slot in range(SENT):
            for at in range(tiles):
                stage_copy(slot, at).wait_recv()


def early_call(pipes, ranks, starts, query, grad, key, panel, inputs):
    length, width = query.shape
    slim = key.shape[1]
    columns = panel.shape[1]
    kv_heads = slim // HD
    groups = width // slim
    rows = length // BLOCKS
    lanes = heads_together(rows, groups) * rows
    tile = math.gcd(width, 1024)
    tiles = width // tile
    kept = length - SENT * rows
    reaches = [(at + 1) * rows for at in range(BLOCKS)]
    probs_shapes = [(kv_heads, reach, groups * rows) for reach in reaches]
    others = max(ranks - 1, 1)
    any_spec = pl.BlockSpec(memory_space=pl.ANY)
    dma = pltpu.SemaphoreType.DMA
    shape = jax.ShapeDtypeStruct
    scratch = [pltpu.VMEM((reach, lanes), WIDE) for reach in reaches]
    scratch += [pltpu.VMEM(probs_shape, LOW) for probs_shape in probs_shapes]
    scratch += [pltpu.VMEM((rows, slim), LOW) for _ in range(BLOCKS)]
    scratch += [pltpu.VMEM((others, rows, slim), LOW) for _ in range(BLOCKS)]
    scratch += [
        pltpu.VMEM(starts.shape, starts.dtype),
        pltpu.VMEM(query.shape, LOW),
        pltpu.VMEM(query.shape, LOW),
        pltpu.VMEM(key.shape, LOW),
        pltpu.VMEM(panel.shape, LOW),
        pltpu.VMEM(inputs.shape, LOW),
        pltpu.VMEM((length, slim), WIDE),
        pltpu.VMEM((length, columns), LOW),
        pltpu.VMEM((length, width), LOW),
        pltpu.VMEM((rows, tile), LOW),
        pltpu.VMEM((length, slim), WIDE),
        pltpu.VMEM((others, length, slim), LOW),
        pltpu.VMEM((others, length, slim), LOW),
        pltpu.VMEM((length, slim), LOW),
        dma((3 + 2 * BLOCKS,)),
        dma((tiles,)),
        dma((BLOCKS + 4,)),
        dma((BLOCKS, others)),
        dma((BLOCKS, others)),
        dma((others,)),
        dma((others,)),
        dma((SENT, tiles)),
        dma((SENT, tiles)),
    ]
    return pl.pallas_call(
        functools.partial(early_kernel, pipes, ranks, groups, tile),
        in_specs=[any_spec] * 6,
        out_specs=[any_spec] * (4 + BLOCKS),
        out_shape=[
            shape((SENT * rows, width), LOW),
            shape((kept, width), LOW),
            shape((length, columns), LOW),
            shape(key.shape, LOW),
        ]
        + [shape(probs_shape, LOW) for probs_shape in probs_shapes],
        scratch_shapes=scratch,
        compiler_params=pltpu.CompilerParams(
            collective_id=0, has_side_effects=True, vmem_limit_bytes=60 * 2**20
        ),
        name="probs_and_input_grad",
    )(starts, query, grad, key, panel, inputs)


def weight_kernel(inputs_ref, grad_all_ref, came_ref, weight_ref, joined_ref):
    joined_ref[...] = came_ref[...]
    result = times(inputs_ref[...], grad_all_ref[...], ((0,), (0,)))
    weight_ref[...] = result.astype(weight_ref.dtype)


def weight_call(inputs, grad_all, came):
    length, width = inputs.shape
    columns = grad_all.shape[1]
    tile = math.gcd(width, 1024)
    sent = came.shape[0]
    below = length // sent - 1
    return pl.pallas_call(
        weight_kernel,
        grid=(width // tile,),
        in_specs=[
            pl.BlockSpec((length, tile), lambda at: (0, at)),
            pl.BlockSpec((length, columns), lambda at: (0, 0)),
            pl.BlockSpec((sent, tile), lambda at: (0, at)),
        ],
        out_specs=[
            pl.BlockSpec((tile, columns), lambda at: (at, 0)),
            pl.BlockSpec((sent, tile), lambda at: (below, at)),
        ],
        out_shape=[
            jax.ShapeDtypeStruct((width, columns), LOW),
            jax.ShapeDtypeStruct((length, width), LOW),
        ],
        compiler_params=pltpu.CompilerParams(vmem_limit_bytes=60 * 2**20),
        cost_estimate=pl.CostEstimate(
            flops=2 * length * width * columns, bytes_accessed=2 * width * columns, transcendentals=0
        ),
        name="weight_grad",
    )(inputs, grad_all, came)


def grads_kernel(groups, query_ref, grad_ref, key_ref, value_ref, *others):
    probs, others = others[:BLOCKS], others[BLOCKS:]
    grad_query_ref, grad_key_ref, total, scores = others
    length = query_ref.shape[0]
    rows = length // BLOCKS
    together = heads_together(rows, groups)
    lanes = together * rows
    for at in range(BLOCKS - 1, -1, -1):
        reach = (at + 1) * rows
        at_rows = slice(at * rows, reach)
        for part in range(groups // together):
            columns = slice(part * lanes, (part + 1) * lanes)
            grad_h = stacked(grad_ref, at_rows, part * together, together)
            grad_probs = times(value_ref[:reach, :], grad_h, ((1,), (1,)))
            probs_low = probs[at][0, :, columns].astype(WIDE)
            delta = jnp.sum(probs_low * grad_probs, axis=0, keepdims=True)
            scaled_low = (probs_low * (grad_probs - delta) * SCALING).astype(LOW)
            scores[:reach, columns] = scaled_low
        grad_h = times(scores[:reach, :], key_ref[:reach, :], ((0,), (0,))).astype(LOW)
        for head in range(groups):
            column = slice(head * HD, (head + 1) * HD)
            grad_query_ref[at_rows, column] = grad_h[head * rows : (head + 1) * rows, :]
        query_h = stacked(query_ref, at_rows, 0, groups)
        term = times(scores[:reach, :], query_h)
        if at == BLOCKS - 1:
            total[:reach, :] = term
        else:
            total[:reach, :] += term
    grad_key_ref[...] = total[...].astype(grad_key_ref.dtype)


def grads_call(query, grad, key, values, probs):
    length, width = query.shape
    kv_heads = key.shape[1] // HD
    wide = width // kv_heads
    groups = wide // HD
    rows = length // BLOCKS
    wide_spec = pl.BlockSpec((length, wide), lambda g: (0, g))
    slim_spec = pl.BlockSpec((length, HD), lambda g: (0, g))
    probs_specs = [pl.BlockSpec((1,) + p.shape[1:], lambda g: (g, 0, 0)) for p in probs]
    pairs = kv_heads * groups * length * length
    return pl.pallas_call(
        functools.partial(grads_kernel, groups),
        grid=(kv_heads,),
        in_specs=[wide_spec, wide_spec, slim_spec, slim_spec] + probs_specs,
        out_specs=[wide_spec, slim_spec],
        out_shape=[
            jax.ShapeDtypeStruct(query.shape, LOW),
            jax.ShapeDtypeStruct(key.shape, LOW),
        ],
        scratch_shapes=[
            pltpu.VMEM((length, HD), WIDE),
            pltpu.VMEM((length, groups * rows), LOW),
        ],
        compiler_params=pltpu.CompilerParams(vmem_limit_bytes=60 * 2**20),
        cost_estimate=pl.CostEstimate(
            flops=pairs * HD * 6, bytes_accessed=8 * query.size, transcendentals=0
        ),
        name="query_key_grad",
    )(query, grad, key, values, *probs)


def shards(pipes, ranks, tokens_x, queries, key_rows, out_grad, value_weight, doc_starts):
    inputs = tokens_x[0]
    query, key, grad = queries[0], key_rows[0], out_grad[0]
    came, rest, grad_all, values, *probs = early_call(
        pipes, ranks, doc_starts, query, grad, key, value_weight[0], inputs
    )
    pairs = [(source, source - 1) for source in range(1, pipes)]
    arrived = lax.ppermute(rest, "pipe", pairs)
    weight_grad, joined = weight_call(inputs, grad_all, came)
    grad_query, grad_key = grads_call(query, grad, key, values, probs)
    joined, grad_query = lax.optimization_barrier((joined, grad_query))
    joined = lax.dynamic_update_slice(joined, arrived, (0, 0))
    return (grad_query[None], grad_key[None], weight_grad[None], joined[None])


def solution(mesh):
    pipes, ranks = mesh.shape["pipe"], mesh.shape["tensor"]
    wide, panel = P("pipe", None, "tensor"), P("pipe", "tensor", None)
    return jax.shard_map(
        functools.partial(shards, pipes, ranks),
        mesh=mesh,
        in_specs=(wide, wide, wide, wide, panel, P("pipe", None)),
        out_specs=(wide, wide, panel, wide),
        check_vma=False,
    )
```

```python
import functools
import math

import jax
import jax.numpy as jnp
from jax import lax
from jax.experimental import pallas as pl
from jax.experimental.pallas import tpu as pltpu
from jax.sharding import PartitionSpec as P

HD = 128
BLOCKS = 4
SENT = 2
SCALING = HD ** (-0.5)
TO_EXP2 = SCALING * math.log2(math.e)
LOW = jnp.bfloat16
WIDE = jnp.float32
MESH = pl.DeviceIdType.MESH


def times(left, right, dims=((1,), (0,))):
    return lax.dot_general(left, right, (dims, ((), ())), preferred_element_type=WIDE)


def stacked(ref, rows, head, count):
    columns = pl.ds(pl.multiple_of(head * HD, HD), count * HD)
    block = ref[rows, columns]
    return jnp.concatenate([block[:, at * HD : (at + 1) * HD] for at in range(count)], axis=0)


def heads_together(rows, groups):
    for count in (2, 3, 4, 6, 8, 12):
        if groups % count == 0 and count * rows % HD == 0 and count * rows >= 256:
            return count
    return groups


def early_kernel(
    pipes,
    ranks,
    groups,
    tile,
    starts_hbm,
    query_hbm,
    grad_hbm,
    key_hbm,
    panel_hbm,
    inputs_hbm,
    came_ref,
    rest_ref,
    grad_all_ref,
    values_ref,
    *others,
):
    probs_out, others = others[:BLOCKS], others[BLOCKS:]
    bias, others = others[:BLOCKS], others[BLOCKS:]
    probs, others = others[:BLOCKS], others[BLOCKS:]
    own, others = others[:BLOCKS], others[BLOCKS:]
    came, others = others[:BLOCKS], others[BLOCKS:]
    (
        starts, query, grad, key, panel, inputs, total, grad_all, stage, zeros,
        part_own, part_send, part_came, values,
        in_sem, panel_sem, out_sem, grad_send, grad_recv, part_sent, part_recv,
        stage_send, stage_recv,
    ) = others
    length, width = query.shape
    slim = key.shape[1]
    kv_heads = slim // HD
    rows = length // BLOCKS
    together = heads_together(rows, groups)
    lanes = together * rows
    tiles = width // tile
    kept = length - SENT * rows
    halves = 2 if kv_heads % 2 == 0 else 1
    kv_half, slim_half = kv_heads // halves, slim // halves
    me_p = lax.axis_index("pipe")
    me_t = lax.axis_index("tensor")

    def block_rows(at):
        return slice(at * rows, (at + 1) * rows)

    barrier = pltpu.get_barrier_semaphore()
    for step in range(1, ranks):
        peer = lax.rem(me_t + step, ranks)
        pl.semaphore_signal(barrier, inc=1, device_id=(me_p, peer), device_id_type=MESH)

    @pl.when(me_p > 0)
    def _():
        pl.semaphore_signal(barrier, inc=1, device_id=(me_p - 1, me_t), device_id_type=MESH)

    @pl.when(me_p < pipes - 1)
    def _():
        pl.semaphore_signal(barrier, inc=1, device_id=(me_p + 1, me_t), device_id_type=MESH)

    def load(source, target, sem):
        return pltpu.make_async_copy(source, target, in_sem.at[sem])

    def load_rows(source, target, at, sem):
        return load(source.at[block_rows(at)], target.at[block_rows(at)], sem + at)

    def load_panel(at):
        part = pl.ds(pl.multiple_of(at * tile, tile), tile)
        return pltpu.make_async_copy(panel_hbm.at[part], panel.at[part], panel_sem.at[at])

    last = BLOCKS - 1
    load(starts_hbm, starts, 0).start()
    load(key_hbm, key, 1).start()
    load_rows(query_hbm, query, last, 3).start()
    load_rows(grad_hbm, grad, last, 3 + BLOCKS).start()
    load(starts_hbm, starts, 0).wait()

    def fill_bias(at):
        shape = bias[at].shape
        token_j = lax.broadcasted_iota(jnp.int32, shape, 0)
        token_i = lax.broadcasted_iota(jnp.int32, (1, rows), 1) + at * rows
        first = starts[:, block_rows(at)]
        token_i = jnp.concatenate([token_i] * together, axis=1)
        first = jnp.concatenate([first] * together, axis=1)
        bias[at][...] = jnp.where((token_j <= token_i) & (token_j >= first), 0.0, -1e30)

    fill_bias(last)
    load(key_hbm, key, 1).wait()
    load_rows(query_hbm, query, last, 3).wait()
    load_rows(grad_hbm, grad, last, 3 + BLOCKS).wait()
    for at in range(tiles):
        load_panel(at).start()
    for at in range(last - 1, -1, -1):
        load_rows(query_hbm, query, at, 3).start()
        load_rows(grad_hbm, grad, at, 3 + BLOCKS).start()
    load(inputs_hbm, inputs, 2).start()

    def softmax(at, head):
        reach = (at + 1) * rows
        column = pl.ds(pl.multiple_of(head * HD, HD), HD)
        key_h = key[:reach, column]
        for part in range(groups // together):
            query_h = stacked(query, block_rows(at), head * groups + part * together, together)
            power = times(key_h, query_h, ((1,), (1,))) * TO_EXP2 + bias[at][...]
            top = jnp.max(power, axis=0, keepdims=True)
            expo = jnp.exp2(power - top)
            inverse = 1.0 / jnp.sum(expo, axis=0, keepdims=True)
            probs[at][head, :, part * lanes : (part + 1) * lanes] = (expo * inverse).astype(LOW)
        grad_h = stacked(grad, block_rows(at), head * groups, groups)
        term = times(probs[at][head], grad_h)
        if at == last:
            total[:reach, column] = term
        else:
            total[:reach, column] += term

    def softmax_heads(at, half):
        @pl.loop(half * kv_half, (half + 1) * kv_half)
        def _(head):
            softmax(at, head)

    def half_columns(rank, half):
        return pl.ds(pl.multiple_of(rank * slim + half * slim_half, HD), slim_half)

    def grad_copy(at, half, step):
        peer = lax.rem(me_t + step, ranks)
        part = slice(half * slim_half, (half + 1) * slim_half)
        return pltpu.make_async_remote_copy(
            src_ref=own[at].at[:, part],
            dst_ref=came[at].at[step - 1, :, part],
            send_sem=grad_send.at[at, half, step - 1],
            recv_sem=grad_recv.at[at, half, step - 1],
            device_id=(me_p, peer),
            device_id_type=MESH,
        )

    def give(at, half):
        part = slice(half * slim_half, (half + 1) * slim_half)
        ready = total[block_rows(at), part].astype(LOW)
        own[at][:, part] = ready
        for step in range(1, ranks):
            grad_copy(at, half, step).start()
        grad_all[block_rows(at), half_columns(me_t, half)] = ready

    def take(at):
        for half in range(halves):
            part = slice(half * slim_half, (half + 1) * slim_half)
            for step in range(1, ranks):
                grad_copy(at, half, step).wait_recv()
                rank = lax.rem(me_t + ranks - step, ranks)
                grad_all[block_rows(at), half_columns(rank, half)] = came[at][step - 1, :, part]

    def probs_copy(at):
        return pltpu.make_async_copy(probs[at], probs_out[at], out_sem.at[at])

    def stage_copy(slot, at):
        part = pl.ds(pl.multiple_of(at * tile, tile), tile)
        first = length - (slot + 1) * rows
        return pltpu.make_async_remote_copy(
            src_ref=stage.at[first : first + rows, part],
            dst_ref=came_ref.at[first - kept : first - kept + rows, part],
            send_sem=stage_send.at[slot, at],
            recv_sem=stage_recv.at[slot, at],
            device_id=(me_p - 1, me_t),
            device_id_type=MESH,
        )

    def input_grad(first, end, slots, panel_wait):
        @pl.loop(0, tiles)
        def _(at):
            if panel_wait:
                load_panel(at).wait()
            part = pl.ds(pl.multiple_of(at * tile, tile), tile)
            result = times(grad_all[first:end, :], panel[part, :], ((1,), (1,)))
            stage[first:end, part] = result.astype(LOW)

            @pl.when(me_p > 0)
            def _():
                for slot in slots:
                    stage_copy(slot, at).start()

    def wait_rows(at):
        load_rows(query_hbm, query, at, 3).wait()
        load_rows(grad_hbm, grad, at, 3 + BLOCKS).wait()

    def part_values(rank, target):
        column = 256 if slim % 256 == 0 else HD
        for at in range(0, slim, column):
            part = pl.ds(pl.multiple_of(rank * slim + at, HD), column)
            target[:, at : at + column] = times(inputs[...], panel[:, part]).astype(target.dtype)

    def part_copy(step):
        peer = lax.rem(me_t + step, ranks)
        return pltpu.make_async_remote_copy(
            src_ref=part_send.at[step - 1],
            dst_ref=part_came.at[step - 1],
            send_sem=part_sent.at[step - 1],
            recv_sem=part_recv.at[step - 1],
            device_id=(me_p, peer),
            device_id_type=MESH,
        )

    softmax_heads(last, 0)
    greeted = ranks - 1 + lax.min(me_p, 1) + lax.min(pipes - 1 - me_p, 1)
    pl.semaphore_wait(barrier, greeted)
    give(last, 0)
    for half in range(1, halves):
        softmax_heads(last, half)
        give(last, half)
    probs_copy(last).start()
    fill_bias(last - 1)
    wait_rows(last - 1)
    softmax_heads(last - 1, 0)
    give(last - 1, 0)
    take(last)
    input_grad(length - rows, length, (0,), True)
    for half in range(1, halves):
        softmax_heads(last - 1, half)
        give(last - 1, half)
    probs_copy(last - 1).start()
    for at in range(last - 2, -1, -1):
        fill_bias(at)
        wait_rows(at)
        for half in range(halves):
            softmax_heads(at, half)
            give(at, half)
        probs_copy(at).start()
    load(inputs_hbm, inputs, 2).wait()
    for step in range(1, ranks):
        part_values(lax.rem(me_t + step, ranks), part_send.at[step - 1])
        part_copy(step).start()
    for at in range(last - 1, -1, -1):
        take(at)
    input_grad(0, length - rows, tuple(range(1, SENT)), False)
    rest_copy = pltpu.make_async_copy(stage.at[:kept], rest_ref, out_sem.at[BLOCKS])
    rest_copy.start()
    all_copy = pltpu.make_async_copy(grad_all, grad_all_ref, out_sem.at[BLOCKS + 1])
    all_copy.start()
    part_values(me_t, part_own)
    sum_all = part_own[...]
    for step in range(1, ranks):
        part_copy(step).wait_recv()
        sum_all = sum_all + part_came[step - 1].astype(WIDE)
    values[...] = sum_all.astype(LOW)
    values_copy = pltpu.make_async_copy(values, values_ref, out_sem.at[BLOCKS + 2])
    values_copy.start()

    @pl.when(me_p == pipes - 1)
    def _():
        zeros[...] = jnp.zeros_like(zeros)
        for slot in range(SENT):
            for at in range(tiles):
                part = slice(at * tile, (at + 1) * tile)
                copy = pltpu.make_async_copy(
                    zeros, came_ref.at[slot * rows : (slot + 1) * rows, part], out_sem.at[BLOCKS + 3]
                )
                copy.start()
                copy.wait()

    rest_copy.wait()
    all_copy.wait()
    values_copy.wait()
    for at in range(BLOCKS):
        probs_copy(at).wait()
        for half in range(halves):
            for step in range(1, ranks):
                grad_copy(at, half, step).wait_send()
    for step in range(1, ranks):
        part_copy(step).wait_send()

    @pl.when(me_p > 0)
    def _():
        for slot in range(SENT):
            for at in range(tiles):
                stage_copy(slot, at).wait_send()

    @pl.when(me_p < pipes - 1)
    def _():
        for slot in range(SENT):
            for at in range(tiles):
                stage_copy(slot, at).wait_recv()


def early_call(pipes, ranks, starts, query, grad, key, panel, inputs):
    length, width = query.shape
    slim = key.shape[1]
    columns = panel.shape[1]
    kv_heads = slim // HD
    groups = width // slim
    rows = length // BLOCKS
    lanes = heads_together(rows, groups) * rows
    tile = math.gcd(width, 1024)
    tiles = width // tile
    kept = length - SENT * rows
    reaches = [(at + 1) * rows for at in range(BLOCKS)]
    probs_shapes = [(kv_heads, reach, groups * rows) for reach in reaches]
    others = max(ranks - 1, 1)
    any_spec = pl.BlockSpec(memory_space=pl.ANY)
    dma = pltpu.SemaphoreType.DMA
    shape = jax.ShapeDtypeStruct
    scratch = [pltpu.VMEM((reach, lanes), WIDE) for reach in reaches]
    scratch += [pltpu.VMEM(probs_shape, LOW) for probs_shape in probs_shapes]
    scratch += [pltpu.VMEM((rows, slim), LOW) for _ in range(BLOCKS)]
    scratch += [pltpu.VMEM((others, rows, slim), LOW) for _ in range(BLOCKS)]
    scratch += [
        pltpu.VMEM(starts.shape, starts.dtype),
        pltpu.VMEM(query.shape, LOW),
        pltpu.VMEM(query.shape, LOW),
        pltpu.VMEM(key.shape, LOW),
        pltpu.VMEM(panel.shape, LOW),
        pltpu.VMEM(inputs.shape, LOW),
        pltpu.VMEM((length, slim), WIDE),
        pltpu.VMEM((length, columns), LOW),
        pltpu.VMEM((length, width), LOW),
        pltpu.VMEM((rows, tile), LOW),
        pltpu.VMEM((length, slim), WIDE),
        pltpu.VMEM((others, length, slim), LOW),
        pltpu.VMEM((others, length, slim), LOW),
        pltpu.VMEM((length, slim), LOW),
        dma((3 + 2 * BLOCKS,)),
        dma((tiles,)),
        dma((BLOCKS + 4,)),
        dma((BLOCKS, 2, others)),
        dma((BLOCKS, 2, others)),
        dma((others,)),
        dma((others,)),
        dma((SENT, tiles)),
        dma((SENT, tiles)),
    ]
    return pl.pallas_call(
        functools.partial(early_kernel, pipes, ranks, groups, tile),
        in_specs=[any_spec] * 6,
        out_specs=[any_spec] * (4 + BLOCKS),
        out_shape=[
            shape((SENT * rows, width), LOW),
            shape((kept, width), LOW),
            shape((length, columns), LOW),
            shape(key.shape, LOW),
        ]
        + [shape(probs_shape, LOW) for probs_shape in probs_shapes],
        scratch_shapes=scratch,
        compiler_params=pltpu.CompilerParams(
            collective_id=0, has_side_effects=True, vmem_limit_bytes=60 * 2**20
        ),
        name="probs_and_input_grad",
    )(starts, query, grad, key, panel, inputs)


def late_kernel(
    groups, tile, inputs_hbm, grad_all_hbm, came_hbm, query_hbm, grad_hbm, key_hbm, values_hbm, *others
):
    probs_hbm, others = others[:BLOCKS], others[BLOCKS:]
    weight_hbm, grad_query_hbm, grad_key_hbm, joined_hbm, *others = others
    probs, others = others[:BLOCKS], others[BLOCKS:]
    (
        inputs, grad_all, came, query, grad, key, values, weight, grad_query, grad_key,
        total, scores, in_sem, inputs_sem, weight_sem, query_sem, grad_sem, probs_sem,
        grad_query_sem, out_sem,
    ) = others
    length, width = query.shape
    rows = length // BLOCKS
    kv_heads = key.shape[1] // HD
    wide = groups * HD
    kept = length - came.shape[0]
    tiles = width // tile
    together = heads_together(rows, groups)
    lanes = together * rows
    copy = pltpu.make_async_copy

    def span(at, size):
        return pl.ds(pl.multiple_of(at * size, size), size)

    def load_inputs(at):
        return copy(
            inputs_hbm.at[:, span(at, tile)], inputs.at[:, span(at, tile)], inputs_sem.at[at]
        )

    def store_weight(at):
        return copy(weight.at[span(at, tile)], weight_hbm.at[span(at, tile)], weight_sem.at[at])

    def load_head(head):
        part = span(head, wide)
        copies = [
            copy(query_hbm.at[:, part], query.at[:, part], query_sem.at[head]),
            copy(grad_hbm.at[:, part], grad.at[:, part], grad_sem.at[head]),
        ]
        return copies + [
            copy(probs_hbm[at].at[head], probs[at].at[head], probs_sem.at[at, head])
            for at in range(BLOCKS)
        ]

    def store_head(head):
        part = span(head, wide)
        return copy(grad_query.at[:, part], grad_query_hbm.at[:, part], grad_query_sem.at[head])

    load_all = copy(grad_all_hbm, grad_all, in_sem.at[0])
    load_came = copy(came_hbm, came, in_sem.at[1])
    load_key = copy(key_hbm, key, in_sem.at[2])
    load_values = copy(values_hbm, values, in_sem.at[3])
    load_all.start()
    for at in range(tiles):
        load_inputs(at).start()
    load_came.start()
    load_all.wait()
    load_inputs(0).wait()
    load_key.start()
    load_values.start()
    for head in range(kv_heads):
        for one in load_head(head):
            one.start()

    @pl.loop(0, tiles)
    def _(at):
        @pl.when(at > 0)
        def _():
            load_inputs(at).wait()

        result = times(inputs[:, span(at, tile)], grad_all[...], ((0,), (0,)))
        weight[span(at, tile), :] = result.astype(LOW)
        store_weight(at).start()

    load_came.wait()
    store_came = copy(came, joined_hbm.at[kept:], out_sem.at[0])
    store_came.start()
    load_key.wait()
    load_values.wait()

    @pl.loop(0, kv_heads)
    def _(head):
        for one in load_head(head):
            one.wait()
        column = span(head, HD)
        for at in range(BLOCKS - 1, -1, -1):
            reach = (at + 1) * rows
            at_rows = slice(at * rows, reach)
            for part in range(groups // together):
                columns = slice(part * lanes, (part + 1) * lanes)
                grad_h = stacked(grad, at_rows, head * groups + part * together, together)
                grad_probs = times(values[:reach, column], grad_h, ((1,), (1,)))
                probs_low = probs[at][head, :, columns].astype(WIDE)
                delta = jnp.sum(probs_low * grad_probs, axis=0, keepdims=True)
                scaled_low = (probs_low * (grad_probs - delta) * SCALING).astype(LOW)
                scores[:reach, columns] = scaled_low
            turned = times(scores[:reach, :], key[:reach, column], ((0,), (0,))).astype(LOW)
            for one in range(groups):
                grad_query[at_rows, span(head * groups + one, HD)] = turned[
                    one * rows : (one + 1) * rows, :
                ]
            query_h = stacked(query, at_rows, head * groups, groups)
            term = times(scores[:reach, :], query_h)
            if at == BLOCKS - 1:
                total[:reach, :] = term
            else:
                total[:reach, :] += term
        grad_key[:, column] = total[...].astype(LOW)
        store_head(head).start()

    store_key = copy(grad_key, grad_key_hbm, out_sem.at[1])
    store_key.start()
    store_came.wait()
    store_key.wait()
    for at in range(tiles):
        store_weight(at).wait()
    for head in range(kv_heads):
        store_head(head).wait()


def late_call(inputs, grad_all, came, query, grad, key, values, probs):
    length, width = query.shape
    columns = grad_all.shape[1]
    kv_heads = key.shape[1] // HD
    groups = width // key.shape[1]
    rows = length // BLOCKS
    tile = math.gcd(width, 2048)
    tiles = width // tile
    any_spec = pl.BlockSpec(memory_space=pl.ANY)
    dma = pltpu.SemaphoreType.DMA
    shape = jax.ShapeDtypeStruct
    scratch = [pltpu.VMEM(one.shape, LOW) for one in probs]
    scratch += [
        pltpu.VMEM(one.shape, LOW) for one in (inputs, grad_all, came, query, grad, key, values)
    ]
    scratch += [
        pltpu.VMEM((width, columns), LOW),
        pltpu.VMEM(query.shape, LOW),
        pltpu.VMEM(key.shape, LOW),
        pltpu.VMEM((length, HD), WIDE),
        pltpu.VMEM((length, groups * rows), LOW),
        dma((4,)),
        dma((tiles,)),
        dma((tiles,)),
        dma((kv_heads,)),
        dma((kv_heads,)),
        dma((BLOCKS, kv_heads)),
        dma((kv_heads,)),
        dma((2,)),
    ]
    pairs = kv_heads * groups * length * length
    return pl.pallas_call(
        functools.partial(late_kernel, groups, tile),
        in_specs=[any_spec] * (7 + BLOCKS),
        out_specs=[any_spec] * 4,
        out_shape=[
            shape((width, columns), LOW),
            shape(query.shape, LOW),
            shape(key.shape, LOW),
            shape(query.shape, LOW),
        ],
        scratch_shapes=scratch,
        compiler_params=pltpu.CompilerParams(vmem_limit_bytes=60 * 2**20),
        cost_estimate=pl.CostEstimate(
            flops=pairs * HD * 6 + 2 * length * width * columns,
            bytes_accessed=12 * query.size + 2 * width * columns,
            transcendentals=0,
        ),
        name="weight_query_key_grads",
    )(inputs, grad_all, came, query, grad, key, values, *probs)


def shards(pipes, ranks, tokens_x, queries, key_rows, out_grad, value_weight, doc_starts):
    inputs = tokens_x[0]
    query, key, grad = queries[0], key_rows[0], out_grad[0]
    came, rest, grad_all, values, *probs = early_call(
        pipes, ranks, doc_starts, query, grad, key, value_weight[0], inputs
    )
    pairs = [(source, source - 1) for source in range(1, pipes)]
    arrived = lax.ppermute(rest, "pipe", pairs)
    weight_grad, grad_query, grad_key, joined = late_call(
        inputs, grad_all, came, query, grad, key, values, probs
    )
    joined = lax.dynamic_update_slice(joined, arrived, (0, 0))
    return (grad_query[None], grad_key[None], weight_grad[None], joined[None])


def solution(mesh):
    pipes, ranks = mesh.shape["pipe"], mesh.shape["tensor"]
    wide, panel = P("pipe", None, "tensor"), P("pipe", "tensor", None)
    return jax.shard_map(
        functools.partial(shards, pipes, ranks),
        mesh=mesh,
        in_specs=(wide, wide, wide, wide, panel, P("pipe", None)),
        out_specs=(wide, wide, panel, wide),
        check_vma=False,
    )
```

```python
import functools
import math

import jax
import jax.numpy as jnp
from jax import lax
from jax.experimental import pallas as pl
from jax.experimental.pallas import tpu as pltpu
from jax.sharding import PartitionSpec as P

HD = 128
BLOCKS = 4
SENT = 2
SCALING = HD ** (-0.5)
TO_EXP2 = SCALING * math.log2(math.e)
LOW = jnp.bfloat16
WIDE = jnp.float32
MESH = pl.DeviceIdType.MESH


def times(left, right, dims=((1,), (0,))):
    return lax.dot_general(left, right, (dims, ((), ())), preferred_element_type=WIDE)


def stacked(ref, rows, head, count):
    columns = pl.ds(pl.multiple_of(head * HD, HD), count * HD)
    block = ref[rows, columns]
    return jnp.concatenate([block[:, at * HD : (at + 1) * HD] for at in range(count)], axis=0)


def heads_together(rows, groups):
    for count in (2, 3, 4, 6, 8, 12):
        if groups % count == 0 and count * rows % HD == 0 and count * rows >= 256:
            return count
    return groups


def early_kernel(
    pipes,
    ranks,
    groups,
    tile,
    starts_hbm,
    query_hbm,
    grad_hbm,
    key_hbm,
    panel_hbm,
    inputs_hbm,
    came_ref,
    rest_ref,
    grad_all_ref,
    values_ref,
    *others,
):
    probs_out, others = others[:BLOCKS], others[BLOCKS:]
    bias, others = others[:BLOCKS], others[BLOCKS:]
    probs, others = others[:BLOCKS], others[BLOCKS:]
    own, others = others[:BLOCKS], others[BLOCKS:]
    came, others = others[:BLOCKS], others[BLOCKS:]
    (
        starts, query, grad, key, panel, inputs, total, grad_all, stage, zeros,
        part_own, part_send, part_came, values,
        in_sem, panel_sem, out_sem, grad_send, grad_recv, part_sent, part_recv,
        stage_send, stage_recv,
    ) = others
    length, width = query.shape
    slim = key.shape[1]
    kv_heads = slim // HD
    rows = length // BLOCKS
    together = heads_together(rows, groups)
    lanes = together * rows
    tiles = width // tile
    kept = length - SENT * rows
    halves = math.gcd(kv_heads, 4)
    kv_half, slim_half = kv_heads // halves, slim // halves
    me_p = lax.axis_index("pipe")
    me_t = lax.axis_index("tensor")

    def block_rows(at):
        return slice(at * rows, (at + 1) * rows)

    barrier = pltpu.get_barrier_semaphore()
    for step in range(1, ranks):
        peer = lax.rem(me_t + step, ranks)
        pl.semaphore_signal(barrier, inc=1, device_id=(me_p, peer), device_id_type=MESH)

    @pl.when(me_p > 0)
    def _():
        pl.semaphore_signal(barrier, inc=1, device_id=(me_p - 1, me_t), device_id_type=MESH)

    @pl.when(me_p < pipes - 1)
    def _():
        pl.semaphore_signal(barrier, inc=1, device_id=(me_p + 1, me_t), device_id_type=MESH)

    def load(source, target, sem):
        return pltpu.make_async_copy(source, target, in_sem.at[sem])

    def load_rows(source, target, at, sem):
        return load(source.at[block_rows(at)], target.at[block_rows(at)], sem + at)

    def load_panel(at):
        part = pl.ds(pl.multiple_of(at * tile, tile), tile)
        return pltpu.make_async_copy(panel_hbm.at[part], panel.at[part], panel_sem.at[at])

    last = BLOCKS - 1
    load(starts_hbm, starts, 0).start()
    load(key_hbm, key, 1).start()

    def load_last(half):
        part = slice(half * (width // halves), (half + 1) * (width // halves))
        at = 3 + 2 * BLOCKS + 2 * half
        return (
            load(query_hbm.at[block_rows(last), part], query.at[block_rows(last), part], at),
            load(grad_hbm.at[block_rows(last), part], grad.at[block_rows(last), part], at + 1),
        )

    for half in range(halves):
        for copy in load_last(half):
            copy.start()
    load(starts_hbm, starts, 0).wait()

    def fill_bias(at):
        shape = bias[at].shape
        token_j = lax.broadcasted_iota(jnp.int32, shape, 0)
        token_i = lax.broadcasted_iota(jnp.int32, (1, rows), 1) + at * rows
        first = starts[:, block_rows(at)]
        token_i = jnp.concatenate([token_i] * together, axis=1)
        first = jnp.concatenate([first] * together, axis=1)
        bias[at][...] = jnp.where((token_j <= token_i) & (token_j >= first), 0.0, -1e30)

    fill_bias(last)
    load(key_hbm, key, 1).wait()
    for copy in load_last(0):
        copy.wait()
    for at in range(tiles):
        load_panel(at).start()
    for at in range(last - 1, -1, -1):
        load_rows(query_hbm, query, at, 3).start()
        load_rows(grad_hbm, grad, at, 3 + BLOCKS).start()
    load(inputs_hbm, inputs, 2).start()

    def softmax(at, head):
        reach = (at + 1) * rows
        column = pl.ds(pl.multiple_of(head * HD, HD), HD)
        key_h = key[:reach, column]
        for part in range(groups // together):
            query_h = stacked(query, block_rows(at), head * groups + part * together, together)
            power = times(key_h, query_h, ((1,), (1,))) * TO_EXP2 + bias[at][...]
            top = jnp.max(power, axis=0, keepdims=True)
            expo = jnp.exp2(power - top)
            inverse = 1.0 / jnp.sum(expo, axis=0, keepdims=True)
            probs[at][head, :, part * lanes : (part + 1) * lanes] = (expo * inverse).astype(LOW)
        grad_h = stacked(grad, block_rows(at), head * groups, groups)
        term = times(probs[at][head], grad_h)
        if at == last:
            total[:reach, column] = term
        else:
            total[:reach, column] += term

    def softmax_heads(at, half):
        @pl.loop(half * kv_half, (half + 1) * kv_half)
        def _(head):
            softmax(at, head)

    def half_columns(rank, half):
        return pl.ds(pl.multiple_of(rank * slim + half * slim_half, HD), slim_half)

    def grad_copy(at, half, step):
        peer = lax.rem(me_t + step, ranks)
        part = slice(half * slim_half, (half + 1) * slim_half)
        return pltpu.make_async_remote_copy(
            src_ref=own[at].at[:, part],
            dst_ref=came[at].at[step - 1, :, part],
            send_sem=grad_send.at[at, half, step - 1],
            recv_sem=grad_recv.at[at, half, step - 1],
            device_id=(me_p, peer),
            device_id_type=MESH,
        )

    def give(at, half):
        part = slice(half * slim_half, (half + 1) * slim_half)
        ready = total[block_rows(at), part].astype(LOW)
        own[at][:, part] = ready
        for step in range(1, ranks):
            grad_copy(at, half, step).start()
        grad_all[block_rows(at), half_columns(me_t, half)] = ready

    def take(at):
        for half in range(halves):
            part = slice(half * slim_half, (half + 1) * slim_half)
            for step in range(1, ranks):
                grad_copy(at, half, step).wait_recv()
                rank = lax.rem(me_t + ranks - step, ranks)
                grad_all[block_rows(at), half_columns(rank, half)] = came[at][step - 1, :, part]

    def probs_copy(at):
        return pltpu.make_async_copy(probs[at], probs_out[at], out_sem.at[at])

    def tile_part(at):
        return pl.ds(pl.multiple_of(at * tile, tile), tile)

    def stage_copy(slot, part, at):
        first = length - (slot + 1) * rows
        return pltpu.make_async_remote_copy(
            src_ref=stage.at[first : first + rows, part],
            dst_ref=came_ref.at[first - kept : first - kept + rows, part],
            send_sem=stage_send.at[slot, at],
            recv_sem=stage_recv.at[slot, at],
            device_id=(me_p - 1, me_t),
            device_id_type=MESH,
        )

    half_tile = tile // 2
    pieces = [(slice(0, half_tile), 0), (slice(half_tile, tile), tiles)]

    def all_pieces(slot):
        copies = [stage_copy(slot, part, at) for part, at in pieces]
        return copies + [stage_copy(slot, tile_part(at), at) for at in range(1, tiles)]

    def input_grad_part(first, end, slots, part, at):
        result = times(grad_all[first:end, :], panel[part, :], ((1,), (1,)))
        stage[first:end, part] = result.astype(LOW)

        @pl.when(me_p > 0)
        def _():
            for slot in slots:
                stage_copy(slot, part, at).start()

    def input_grad(first, end, slots, panel_wait):
        if panel_wait:
            load_panel(0).wait()
        for part, at in pieces:
            input_grad_part(first, end, slots, part, at)

        @pl.loop(1, tiles)
        def _(at):
            if panel_wait:
                load_panel(at).wait()
            input_grad_part(first, end, slots, tile_part(at), at)

    def wait_rows(at):
        load_rows(query_hbm, query, at, 3).wait()
        load_rows(grad_hbm, grad, at, 3 + BLOCKS).wait()

    def part_values(rank, target):
        column = 256 if slim % 256 == 0 else HD
        for at in range(0, slim, column):
            part = pl.ds(pl.multiple_of(rank * slim + at, HD), column)
            target[:, at : at + column] = times(inputs[...], panel[:, part]).astype(target.dtype)

    def part_copy(step):
        peer = lax.rem(me_t + step, ranks)
        return pltpu.make_async_remote_copy(
            src_ref=part_send.at[step - 1],
            dst_ref=part_came.at[step - 1],
            send_sem=part_sent.at[step - 1],
            recv_sem=part_recv.at[step - 1],
            device_id=(me_p, peer),
            device_id_type=MESH,
        )

    softmax_heads(last, 0)
    greeted = ranks - 1 + lax.min(me_p, 1) + lax.min(pipes - 1 - me_p, 1)
    pl.semaphore_wait(barrier, greeted)
    give(last, 0)
    for half in range(1, halves):
        for copy in load_last(half):
            copy.wait()
        softmax_heads(last, half)
        give(last, half)
    probs_copy(last).start()
    fill_bias(last - 1)
    wait_rows(last - 1)
    early = max(3 * halves // 4, 1)
    for half in range(early):
        softmax_heads(last - 1, half)
        give(last - 1, half)
    take(last)
    input_grad(length - rows, length, (0,), True)
    for half in range(early, halves):
        softmax_heads(last - 1, half)
        give(last - 1, half)
    probs_copy(last - 1).start()
    for at in range(last - 2, -1, -1):
        fill_bias(at)
        wait_rows(at)
        for half in range(halves):
            softmax_heads(at, half)
            give(at, half)
        probs_copy(at).start()
    load(inputs_hbm, inputs, 2).wait()
    for step in range(1, ranks):
        part_values(lax.rem(me_t + step, ranks), part_send.at[step - 1])
        part_copy(step).start()
    for at in range(last - 1, -1, -1):
        take(at)
    input_grad(0, length - rows, tuple(range(1, SENT)), False)
    rest_copy = pltpu.make_async_copy(stage.at[:kept], rest_ref, out_sem.at[BLOCKS])
    rest_copy.start()
    all_copy = pltpu.make_async_copy(grad_all, grad_all_ref, out_sem.at[BLOCKS + 1])
    all_copy.start()
    part_values(me_t, part_own)
    sum_all = part_own[...]
    for step in range(1, ranks):
        part_copy(step).wait_recv()
        sum_all = sum_all + part_came[step - 1].astype(WIDE)
    values[...] = sum_all.astype(LOW)
    values_copy = pltpu.make_async_copy(values, values_ref, out_sem.at[BLOCKS + 2])
    values_copy.start()

    @pl.when(me_p == pipes - 1)
    def _():
        zeros[...] = jnp.zeros_like(zeros)
        for slot in range(SENT):
            for at in range(tiles):
                part = slice(at * tile, (at + 1) * tile)
                copy = pltpu.make_async_copy(
                    zeros, came_ref.at[slot * rows : (slot + 1) * rows, part], out_sem.at[BLOCKS + 3]
                )
                copy.start()
                copy.wait()

    rest_copy.wait()
    all_copy.wait()
    values_copy.wait()
    for at in range(BLOCKS):
        probs_copy(at).wait()
        for half in range(halves):
            for step in range(1, ranks):
                grad_copy(at, half, step).wait_send()
    for step in range(1, ranks):
        part_copy(step).wait_send()

    @pl.when(me_p > 0)
    def _():
        for slot in range(SENT):
            for copy in all_pieces(slot):
                copy.wait_send()

    @pl.when(me_p < pipes - 1)
    def _():
        for slot in range(SENT):
            for copy in all_pieces(slot):
                copy.wait_recv()


def early_call(pipes, ranks, starts, query, grad, key, panel, inputs):
    length, width = query.shape
    slim = key.shape[1]
    columns = panel.shape[1]
    kv_heads = slim // HD
    groups = width // slim
    rows = length // BLOCKS
    lanes = heads_together(rows, groups) * rows
    tile = math.gcd(width, 1024)
    tiles = width // tile
    kept = length - SENT * rows
    reaches = [(at + 1) * rows for at in range(BLOCKS)]
    probs_shapes = [(kv_heads, reach, groups * rows) for reach in reaches]
    others = max(ranks - 1, 1)
    any_spec = pl.BlockSpec(memory_space=pl.ANY)
    dma = pltpu.SemaphoreType.DMA
    shape = jax.ShapeDtypeStruct
    scratch = [pltpu.VMEM((reach, lanes), WIDE) for reach in reaches]
    scratch += [pltpu.VMEM(probs_shape, LOW) for probs_shape in probs_shapes]
    scratch += [pltpu.VMEM((rows, slim), LOW) for _ in range(BLOCKS)]
    scratch += [pltpu.VMEM((others, rows, slim), LOW) for _ in range(BLOCKS)]
    scratch += [
        pltpu.VMEM(starts.shape, starts.dtype),
        pltpu.VMEM(query.shape, LOW),
        pltpu.VMEM(query.shape, LOW),
        pltpu.VMEM(key.shape, LOW),
        pltpu.VMEM(panel.shape, LOW),
        pltpu.VMEM(inputs.shape, LOW),
        pltpu.VMEM((length, slim), WIDE),
        pltpu.VMEM((length, columns), LOW),
        pltpu.VMEM((length, width), LOW),
        pltpu.VMEM((rows, tile), LOW),
        pltpu.VMEM((length, slim), WIDE),
        pltpu.VMEM((others, length, slim), LOW),
        pltpu.VMEM((others, length, slim), LOW),
        pltpu.VMEM((length, slim), LOW),
        dma((3 + 2 * BLOCKS + 8,)),
        dma((tiles,)),
        dma((BLOCKS + 4,)),
        dma((BLOCKS, 4, others)),
        dma((BLOCKS, 4, others)),
        dma((others,)),
        dma((others,)),
        dma((SENT, tiles + 1)),
        dma((SENT, tiles + 1)),
    ]
    return pl.pallas_call(
        functools.partial(early_kernel, pipes, ranks, groups, tile),
        in_specs=[any_spec] * 6,
        out_specs=[any_spec] * (4 + BLOCKS),
        out_shape=[
            shape((SENT * rows, width), LOW),
            shape((kept, width), LOW),
            shape((length, columns), LOW),
            shape(key.shape, LOW),
        ]
        + [shape(probs_shape, LOW) for probs_shape in probs_shapes],
        scratch_shapes=scratch,
        compiler_params=pltpu.CompilerParams(
            collective_id=0, has_side_effects=True, vmem_limit_bytes=60 * 2**20
        ),
        name="probs_and_input_grad",
    )(starts, query, grad, key, panel, inputs)


def late_kernel(
    groups, tile, inputs_hbm, grad_all_hbm, came_hbm, query_hbm, grad_hbm, key_hbm, values_hbm, *others
):
    probs_hbm, others = others[:BLOCKS], others[BLOCKS:]
    weight_hbm, grad_query_hbm, grad_key_hbm, joined_hbm, *others = others
    probs, others = others[:BLOCKS], others[BLOCKS:]
    (
        inputs, grad_all, came, query, grad, key, values, weight, grad_query, grad_key,
        total, scores, in_sem, inputs_sem, weight_sem, query_sem, grad_sem, probs_sem,
        grad_query_sem, out_sem,
    ) = others
    length, width = query.shape
    rows = length // BLOCKS
    kv_heads = key.shape[1] // HD
    wide = groups * HD
    kept = length - came.shape[0]
    tiles = width // tile
    together = heads_together(rows, groups)
    lanes = together * rows
    copy = pltpu.make_async_copy

    def span(at, size):
        return pl.ds(pl.multiple_of(at * size, size), size)

    def load_inputs(at):
        return copy(
            inputs_hbm.at[:, span(at, tile)], inputs.at[:, span(at, tile)], inputs_sem.at[at]
        )

    def store_weight(at):
        return copy(weight.at[span(at, tile)], weight_hbm.at[span(at, tile)], weight_sem.at[at])

    def load_head(head):
        part = span(head, wide)
        copies = [
            copy(query_hbm.at[:, part], query.at[:, part], query_sem.at[head]),
            copy(grad_hbm.at[:, part], grad.at[:, part], grad_sem.at[head]),
        ]
        return copies + [
            copy(probs_hbm[at].at[head], probs[at].at[head], probs_sem.at[at, head])
            for at in range(BLOCKS)
        ]

    def store_head(head):
        part = span(head, wide)
        return copy(grad_query.at[:, part], grad_query_hbm.at[:, part], grad_query_sem.at[head])

    load_all = copy(grad_all_hbm, grad_all, in_sem.at[0])
    load_came = copy(came_hbm, came, in_sem.at[1])
    load_key = copy(key_hbm, key, in_sem.at[2])
    load_values = copy(values_hbm, values, in_sem.at[3])
    load_all.start()
    for at in range(tiles):
        load_inputs(at).start()
    load_came.start()
    load_all.wait()
    load_inputs(0).wait()
    load_key.start()
    load_values.start()
    for head in range(kv_heads):
        for one in load_head(head):
            one.start()

    @pl.loop(0, tiles)
    def _(at):
        @pl.when(at > 0)
        def _():
            load_inputs(at).wait()

        result = times(inputs[:, span(at, tile)], grad_all[...], ((0,), (0,)))
        weight[span(at, tile), :] = result.astype(LOW)
        store_weight(at).start()

    load_came.wait()
    store_came = copy(came, joined_hbm.at[kept:], out_sem.at[0])
    store_came.start()
    load_key.wait()
    load_values.wait()

    @pl.loop(0, kv_heads)
    def _(head):
        for one in load_head(head):
            one.wait()
        column = span(head, HD)
        for at in range(BLOCKS - 1, -1, -1):
            reach = (at + 1) * rows
            at_rows = slice(at * rows, reach)
            for part in range(groups // together):
                columns = slice(part * lanes, (part + 1) * lanes)
                grad_h = stacked(grad, at_rows, head * groups + part * together, together)
                grad_probs = times(values[:reach, column], grad_h, ((1,), (1,)))
                probs_low = probs[at][head, :, columns].astype(WIDE)
                delta = jnp.sum(probs_low * grad_probs, axis=0, keepdims=True)
                scaled_low = (probs_low * (grad_probs - delta) * SCALING).astype(LOW)
                scores[:reach, columns] = scaled_low
            turned = times(scores[:reach, :], key[:reach, column], ((0,), (0,))).astype(LOW)
            for one in range(groups):
                grad_query[at_rows, span(head * groups + one, HD)] = turned[
                    one * rows : (one + 1) * rows, :
                ]
            query_h = stacked(query, at_rows, head * groups, groups)
            term = times(scores[:reach, :], query_h)
            if at == BLOCKS - 1:
                total[:reach, :] = term
            else:
                total[:reach, :] += term
        grad_key[:, column] = total[...].astype(LOW)
        store_head(head).start()

    store_key = copy(grad_key, grad_key_hbm, out_sem.at[1])
    store_key.start()
    store_came.wait()
    store_key.wait()
    for at in range(tiles):
        store_weight(at).wait()
    for head in range(kv_heads):
        store_head(head).wait()


def late_call(inputs, grad_all, came, query, grad, key, values, probs):
    length, width = query.shape
    columns = grad_all.shape[1]
    kv_heads = key.shape[1] // HD
    groups = width // key.shape[1]
    rows = length // BLOCKS
    tile = math.gcd(width, 2048)
    tiles = width // tile
    any_spec = pl.BlockSpec(memory_space=pl.ANY)
    dma = pltpu.SemaphoreType.DMA
    shape = jax.ShapeDtypeStruct
    scratch = [pltpu.VMEM(one.shape, LOW) for one in probs]
    scratch += [
        pltpu.VMEM(one.shape, LOW) for one in (inputs, grad_all, came, query, grad, key, values)
    ]
    scratch += [
        pltpu.VMEM((width, columns), LOW),
        pltpu.VMEM(query.shape, LOW),
        pltpu.VMEM(key.shape, LOW),
        pltpu.VMEM((length, HD), WIDE),
        pltpu.VMEM((length, groups * rows), LOW),
        dma((4,)),
        dma((tiles,)),
        dma((tiles,)),
        dma((kv_heads,)),
        dma((kv_heads,)),
        dma((BLOCKS, kv_heads)),
        dma((kv_heads,)),
        dma((2,)),
    ]
    pairs = kv_heads * groups * length * length
    return pl.pallas_call(
        functools.partial(late_kernel, groups, tile),
        in_specs=[any_spec] * (7 + BLOCKS),
        out_specs=[any_spec] * 4,
        out_shape=[
            shape((width, columns), LOW),
            shape(query.shape, LOW),
            shape(key.shape, LOW),
            shape(query.shape, LOW),
        ],
        scratch_shapes=scratch,
        compiler_params=pltpu.CompilerParams(vmem_limit_bytes=60 * 2**20),
        cost_estimate=pl.CostEstimate(
            flops=pairs * HD * 6 + 2 * length * width * columns,
            bytes_accessed=12 * query.size + 2 * width * columns,
            transcendentals=0,
        ),
        name="weight_query_key_grads",
    )(inputs, grad_all, came, query, grad, key, values, *probs)


def shards(pipes, ranks, tokens_x, queries, key_rows, out_grad, value_weight, doc_starts):
    inputs = tokens_x[0]
    query, key, grad = queries[0], key_rows[0], out_grad[0]
    came, rest, grad_all, values, *probs = early_call(
        pipes, ranks, doc_starts, query, grad, key, value_weight[0], inputs
    )
    pairs = [(source, source - 1) for source in range(1, pipes)]
    arrived = lax.ppermute(rest, "pipe", pairs)
    weight_grad, grad_query, grad_key, joined = late_call(
        inputs, grad_all, came, query, grad, key, values, probs
    )
    joined = lax.dynamic_update_slice(joined, arrived, (0, 0))
    return (grad_query[None], grad_key[None], weight_grad[None], joined[None])


def solution(mesh):
    pipes, ranks = mesh.shape["pipe"], mesh.shape["tensor"]
    wide, panel = P("pipe", None, "tensor"), P("pipe", "tensor", None)
    return jax.shard_map(
        functools.partial(shards, pipes, ranks),
        mesh=mesh,
        in_specs=(wide, wide, wide, wide, panel, P("pipe", None)),
        out_specs=(wide, wide, panel, wide),
        check_vma=False,
    )
```

```python
import functools
import math

import jax
import jax.numpy as jnp
from jax import lax
from jax.experimental import pallas as pl
from jax.experimental.pallas import tpu as pltpu
from jax.sharding import PartitionSpec as P

HD = 128
BLOCKS = 4
SENT = 2
SCALING = HD ** (-0.5)
TO_EXP2 = SCALING * math.log2(math.e)
LOW = jnp.bfloat16
WIDE = jnp.float32
MESH = pl.DeviceIdType.MESH


def times(left, right, dims=((1,), (0,))):
    return lax.dot_general(left, right, (dims, ((), ())), preferred_element_type=WIDE)


def stacked(ref, rows, head, count):
    columns = pl.ds(pl.multiple_of(head * HD, HD), count * HD)
    block = ref[rows, columns]
    return jnp.concatenate([block[:, at * HD : (at + 1) * HD] for at in range(count)], axis=0)


def heads_together(rows, groups):
    for count in (2, 3, 4, 6, 8, 12):
        if groups % count == 0 and count * rows % HD == 0 and count * rows >= 256:
            return count
    return groups


def early_kernel(
    pipes,
    ranks,
    groups,
    tile,
    starts_hbm,
    query_hbm,
    grad_hbm,
    key_hbm,
    panel_hbm,
    inputs_hbm,
    came_ref,
    rest_ref,
    grad_all_ref,
    values_ref,
    *others,
):
    probs_out, others = others[:BLOCKS], others[BLOCKS:]
    bias, others = others[:BLOCKS], others[BLOCKS:]
    probs, others = others[:BLOCKS], others[BLOCKS:]
    own, others = others[:BLOCKS], others[BLOCKS:]
    came, others = others[:BLOCKS], others[BLOCKS:]
    (
        starts, query, grad, key, panel, inputs, total, grad_all, stage, zeros,
        part_own, part_send, part_came, values,
        in_sem, panel_sem, out_sem, grad_send, grad_recv, part_sent, part_recv,
        stage_send, stage_recv,
    ) = others
    length, width = query.shape
    slim = key.shape[1]
    kv_heads = slim // HD
    rows = length // BLOCKS
    together = heads_together(rows, groups)
    lanes = together * rows
    tiles = width // tile
    kept = length - SENT * rows
    halves = math.gcd(kv_heads, 4)
    kv_half, slim_half = kv_heads // halves, slim // halves
    me_p = lax.axis_index("pipe")
    me_t = lax.axis_index("tensor")

    def block_rows(at):
        return slice(at * rows, (at + 1) * rows)

    barrier = pltpu.get_barrier_semaphore()
    for step in range(1, ranks):
        peer = lax.rem(me_t + step, ranks)
        pl.semaphore_signal(barrier, inc=1, device_id=(me_p, peer), device_id_type=MESH)

    @pl.when(me_p > 0)
    def _():
        pl.semaphore_signal(barrier, inc=1, device_id=(me_p - 1, me_t), device_id_type=MESH)

    @pl.when(me_p < pipes - 1)
    def _():
        pl.semaphore_signal(barrier, inc=1, device_id=(me_p + 1, me_t), device_id_type=MESH)

    def load(source, target, sem):
        return pltpu.make_async_copy(source, target, in_sem.at[sem])

    def load_rows(source, target, at, sem):
        return load(source.at[block_rows(at)], target.at[block_rows(at)], sem + at)

    def load_panel(at):
        part = pl.ds(pl.multiple_of(at * tile, tile), tile)
        return pltpu.make_async_copy(panel_hbm.at[part], panel.at[part], panel_sem.at[at])

    last = BLOCKS - 1
    load(starts_hbm, starts, 0).start()
    load(key_hbm, key, 1).start()

    def load_last(half):
        part = slice(half * (width // halves), (half + 1) * (width // halves))
        at = 3 + 2 * BLOCKS + 2 * half
        return (
            load(query_hbm.at[block_rows(last), part], query.at[block_rows(last), part], at),
            load(grad_hbm.at[block_rows(last), part], grad.at[block_rows(last), part], at + 1),
        )

    for half in range(halves):
        for copy in load_last(half):
            copy.start()
    load(starts_hbm, starts, 0).wait()

    def fill_bias(at):
        shape = bias[at].shape
        token_j = lax.broadcasted_iota(jnp.int32, shape, 0)
        token_i = lax.broadcasted_iota(jnp.int32, (1, rows), 1) + at * rows
        first = starts[:, block_rows(at)]
        token_i = jnp.concatenate([token_i] * together, axis=1)
        first = jnp.concatenate([first] * together, axis=1)
        bias[at][...] = jnp.where((token_j <= token_i) & (token_j >= first), 0.0, -1e30)

    fill_bias(last)
    load(key_hbm, key, 1).wait()
    for copy in load_last(0):
        copy.wait()
    for at in range(tiles):
        load_panel(at).start()
    for at in range(last - 1, -1, -1):
        load_rows(query_hbm, query, at, 3).start()
        load_rows(grad_hbm, grad, at, 3 + BLOCKS).start()
    load(inputs_hbm, inputs, 2).start()

    def softmax(at, head):
        reach = (at + 1) * rows
        column = pl.ds(pl.multiple_of(head * HD, HD), HD)
        key_h = key[:reach, column]
        for part in range(groups // together):
            query_h = stacked(query, block_rows(at), head * groups + part * together, together)
            power = times(key_h, query_h, ((1,), (1,))) * TO_EXP2 + bias[at][...]
            top = jnp.max(power, axis=0, keepdims=True)
            expo = jnp.exp2(power - top)
            inverse = 1.0 / jnp.sum(expo, axis=0, keepdims=True)
            probs[at][head, :, part * lanes : (part + 1) * lanes] = (expo * inverse).astype(LOW)
        grad_h = stacked(grad, block_rows(at), head * groups, groups)
        term = times(probs[at][head], grad_h)
        if at == last:
            total[:reach, column] = term
        else:
            total[:reach, column] += term

    def softmax_heads(at, half):
        @pl.loop(half * kv_half, (half + 1) * kv_half)
        def _(head):
            softmax(at, head)

    def half_columns(rank, half):
        return pl.ds(pl.multiple_of(rank * slim + half * slim_half, HD), slim_half)

    def grad_copy(at, half, step):
        peer = lax.rem(me_t + step, ranks)
        part = slice(half * slim_half, (half + 1) * slim_half)
        return pltpu.make_async_remote_copy(
            src_ref=own[at].at[:, part],
            dst_ref=came[at].at[step - 1, :, part],
            send_sem=grad_send.at[at, half, step - 1],
            recv_sem=grad_recv.at[at, half, step - 1],
            device_id=(me_p, peer),
            device_id_type=MESH,
        )

    def give(at, half):
        part = slice(half * slim_half, (half + 1) * slim_half)
        ready = total[block_rows(at), part].astype(LOW)
        own[at][:, part] = ready
        for step in range(1, ranks):
            grad_copy(at, half, step).start()
        grad_all[block_rows(at), half_columns(me_t, half)] = ready

    def take(at):
        for half in range(halves):
            part = slice(half * slim_half, (half + 1) * slim_half)
            for step in range(1, ranks):
                grad_copy(at, half, step).wait_recv()
                rank = lax.rem(me_t + ranks - step, ranks)
                grad_all[block_rows(at), half_columns(rank, half)] = came[at][step - 1, :, part]

    def probs_copy(at):
        return pltpu.make_async_copy(probs[at], probs_out[at], out_sem.at[at])

    def tile_part(at):
        return pl.ds(pl.multiple_of(at * tile, tile), tile)

    def stage_copy(slot, part, at):
        first = length - (slot + 1) * rows
        return pltpu.make_async_remote_copy(
            src_ref=stage.at[first : first + rows, part],
            dst_ref=came_ref.at[first - kept : first - kept + rows, part],
            send_sem=stage_send.at[slot, at],
            recv_sem=stage_recv.at[slot, at],
            device_id=(me_p - 1, me_t),
            device_id_type=MESH,
        )

    half_tile = tile // 2
    pieces = [(slice(0, half_tile), 0), (slice(half_tile, tile), tiles)]

    def all_pieces(slot):
        copies = [stage_copy(slot, part, at) for part, at in pieces]
        return copies + [stage_copy(slot, tile_part(at), at) for at in range(1, tiles)]

    def input_grad_part(first, end, slots, part, at):
        result = times(grad_all[first:end, :], panel[part, :], ((1,), (1,)))
        stage[first:end, part] = result.astype(LOW)

        @pl.when(me_p > 0)
        def _():
            for slot in slots:
                stage_copy(slot, part, at).start()

    def input_grad(first, end, slots, panel_wait):
        if panel_wait:
            load_panel(0).wait()
        for part, at in pieces:
            input_grad_part(first, end, slots, part, at)

        @pl.loop(1, tiles)
        def _(at):
            if panel_wait:
                load_panel(at).wait()
            input_grad_part(first, end, slots, tile_part(at), at)

    def wait_rows(at):
        load_rows(query_hbm, query, at, 3).wait()
        load_rows(grad_hbm, grad, at, 3 + BLOCKS).wait()

    def part_values(rank, target):
        column = 256 if slim % 256 == 0 else HD
        for at in range(0, slim, column):
            part = pl.ds(pl.multiple_of(rank * slim + at, HD), column)
            target[:, at : at + column] = times(inputs[...], panel[:, part]).astype(target.dtype)

    def part_copy(step):
        peer = lax.rem(me_t + step, ranks)
        return pltpu.make_async_remote_copy(
            src_ref=part_send.at[step - 1],
            dst_ref=part_came.at[step - 1],
            send_sem=part_sent.at[step - 1],
            recv_sem=part_recv.at[step - 1],
            device_id=(me_p, peer),
            device_id_type=MESH,
        )

    softmax_heads(last, 0)
    greeted = ranks - 1 + lax.min(me_p, 1) + lax.min(pipes - 1 - me_p, 1)
    pl.semaphore_wait(barrier, greeted)
    give(last, 0)
    for half in range(1, halves):
        for copy in load_last(half):
            copy.wait()
        softmax_heads(last, half)
        give(last, half)
    probs_copy(last).start()
    fill_bias(last - 1)
    wait_rows(last - 1)
    early = max(3 * halves // 4, 1)
    for half in range(early):
        softmax_heads(last - 1, half)
        give(last - 1, half)
    take(last)
    input_grad(length - rows, length, (0,), True)
    for half in range(early, halves):
        softmax_heads(last - 1, half)
        give(last - 1, half)
    probs_copy(last - 1).start()
    for at in range(last - 2, -1, -1):
        fill_bias(at)
        wait_rows(at)
        for half in range(halves):
            softmax_heads(at, half)
            give(at, half)
        probs_copy(at).start()
    load(inputs_hbm, inputs, 2).wait()
    for step in range(1, ranks):
        part_values(lax.rem(me_t + step, ranks), part_send.at[step - 1])
        part_copy(step).start()
    for at in range(last - 1, -1, -1):
        take(at)
    input_grad(0, length - rows, tuple(range(1, SENT)), False)
    rest_copy = pltpu.make_async_copy(stage.at[:kept], rest_ref, out_sem.at[BLOCKS])
    rest_copy.start()
    all_copy = pltpu.make_async_copy(grad_all, grad_all_ref, out_sem.at[BLOCKS + 1])
    all_copy.start()
    part_values(me_t, part_own)
    sum_all = part_own[...]
    for step in range(1, ranks):
        part_copy(step).wait_recv()
        sum_all = sum_all + part_came[step - 1].astype(WIDE)
    values[...] = sum_all.astype(LOW)
    values_copy = pltpu.make_async_copy(values, values_ref, out_sem.at[BLOCKS + 2])
    values_copy.start()

    @pl.when(me_p == pipes - 1)
    def _():
        zeros[...] = jnp.zeros_like(zeros)
        for slot in range(SENT):
            for at in range(tiles):
                part = slice(at * tile, (at + 1) * tile)
                copy = pltpu.make_async_copy(
                    zeros, came_ref.at[slot * rows : (slot + 1) * rows, part], out_sem.at[BLOCKS + 3]
                )
                copy.start()
                copy.wait()

    rest_copy.wait()
    all_copy.wait()
    values_copy.wait()
    for at in range(BLOCKS):
        probs_copy(at).wait()
        for half in range(halves):
            for step in range(1, ranks):
                grad_copy(at, half, step).wait_send()
    for step in range(1, ranks):
        part_copy(step).wait_send()

    @pl.when(me_p > 0)
    def _():
        for slot in range(SENT):
            for copy in all_pieces(slot):
                copy.wait_send()

    @pl.when(me_p < pipes - 1)
    def _():
        for slot in range(SENT):
            for copy in all_pieces(slot):
                copy.wait_recv()


def early_call(pipes, ranks, starts, query, grad, key, panel, inputs):
    length, width = query.shape
    slim = key.shape[1]
    columns = panel.shape[1]
    kv_heads = slim // HD
    groups = width // slim
    rows = length // BLOCKS
    lanes = heads_together(rows, groups) * rows
    tile = math.gcd(width, 1024)
    tiles = width // tile
    kept = length - SENT * rows
    reaches = [(at + 1) * rows for at in range(BLOCKS)]
    probs_shapes = [(kv_heads, reach, groups * rows) for reach in reaches]
    others = max(ranks - 1, 1)
    any_spec = pl.BlockSpec(memory_space=pl.ANY)
    dma = pltpu.SemaphoreType.DMA
    shape = jax.ShapeDtypeStruct
    scratch = [pltpu.VMEM((reach, lanes), WIDE) for reach in reaches]
    scratch += [pltpu.VMEM(probs_shape, LOW) for probs_shape in probs_shapes]
    scratch += [pltpu.VMEM((rows, slim), LOW) for _ in range(BLOCKS)]
    scratch += [pltpu.VMEM((others, rows, slim), LOW) for _ in range(BLOCKS)]
    scratch += [
        pltpu.VMEM(starts.shape, starts.dtype),
        pltpu.VMEM(query.shape, LOW),
        pltpu.VMEM(query.shape, LOW),
        pltpu.VMEM(key.shape, LOW),
        pltpu.VMEM(panel.shape, LOW),
        pltpu.VMEM(inputs.shape, LOW),
        pltpu.VMEM((length, slim), WIDE),
        pltpu.VMEM((length, columns), LOW),
        pltpu.VMEM((length, width), LOW),
        pltpu.VMEM((rows, tile), LOW),
        pltpu.VMEM((length, slim), WIDE),
        pltpu.VMEM((others, length, slim), LOW),
        pltpu.VMEM((others, length, slim), LOW),
        pltpu.VMEM((length, slim), LOW),
        dma((3 + 2 * BLOCKS + 8,)),
        dma((tiles,)),
        dma((BLOCKS + 4,)),
        dma((BLOCKS, 4, others)),
        dma((BLOCKS, 4, others)),
        dma((others,)),
        dma((others,)),
        dma((SENT, tiles + 1)),
        dma((SENT, tiles + 1)),
    ]
    return pl.pallas_call(
        functools.partial(early_kernel, pipes, ranks, groups, tile),
        in_specs=[any_spec] * 6,
        out_specs=[any_spec] * (4 + BLOCKS),
        out_shape=[
            shape((SENT * rows, width), LOW),
            shape((kept, width), LOW),
            shape((length, columns), LOW),
            shape(key.shape, LOW),
        ]
        + [shape(probs_shape, LOW) for probs_shape in probs_shapes],
        scratch_shapes=scratch,
        compiler_params=pltpu.CompilerParams(
            collective_id=0, has_side_effects=True, vmem_limit_bytes=60 * 2**20
        ),
        name="probs_and_input_grad",
    )(starts, query, grad, key, panel, inputs)


def late_kernel(
    groups, tile, inputs_hbm, grad_all_hbm, came_hbm, query_hbm, grad_hbm, key_hbm, values_hbm, *others
):
    probs_hbm, others = others[:BLOCKS], others[BLOCKS:]
    weight_hbm, grad_query_hbm, grad_key_hbm, joined_hbm, *others = others
    probs, others = others[:BLOCKS], others[BLOCKS:]
    (
        inputs, grad_all, came, query, grad, key, values, weight, grad_query, grad_key,
        total, scores, in_sem, inputs_sem, weight_sem, query_sem, grad_sem, probs_sem,
        grad_query_sem, out_sem,
    ) = others
    length, width = query.shape
    rows = length // BLOCKS
    kv_heads = key.shape[1] // HD
    wide = groups * HD
    kept = length - came.shape[0]
    tiles = width // tile
    together = heads_together(rows, groups)
    lanes = together * rows
    copy = pltpu.make_async_copy

    def span(at, size):
        return pl.ds(pl.multiple_of(at * size, size), size)

    def load_inputs(at):
        return copy(
            inputs_hbm.at[:, span(at, tile)], inputs.at[:, span(at, tile)], inputs_sem.at[at]
        )

    def store_weight(at):
        return copy(weight.at[span(at, tile)], weight_hbm.at[span(at, tile)], weight_sem.at[at])

    def load_head(head):
        part = span(head, wide)
        copies = [
            copy(query_hbm.at[:, part], query.at[:, part], query_sem.at[head]),
            copy(grad_hbm.at[:, part], grad.at[:, part], grad_sem.at[head]),
        ]
        return copies + [
            copy(probs_hbm[at].at[head], probs[at].at[head], probs_sem.at[at, head])
            for at in range(BLOCKS)
        ]

    def store_head(head):
        part = span(head, wide)
        return copy(grad_query.at[:, part], grad_query_hbm.at[:, part], grad_query_sem.at[head])

    load_all = copy(grad_all_hbm, grad_all, in_sem.at[0])
    load_came = copy(came_hbm, came, in_sem.at[1])
    load_key = copy(key_hbm, key, in_sem.at[2])
    load_values = copy(values_hbm, values, in_sem.at[3])
    load_all.start()
    for at in range(tiles):
        load_inputs(at).start()
    load_came.start()
    load_all.wait()
    load_inputs(0).wait()
    load_key.start()
    load_values.start()
    for head in range(kv_heads):
        for one in load_head(head):
            one.start()

    @pl.loop(0, tiles)
    def _(at):
        @pl.when(at > 0)
        def _():
            load_inputs(at).wait()

        result = times(inputs[:, span(at, tile)], grad_all[...], ((0,), (0,)))
        weight[span(at, tile), :] = result.astype(LOW)
        store_weight(at).start()

    load_came.wait()
    store_came = copy(came, joined_hbm.at[kept:], out_sem.at[0])
    store_came.start()
    load_key.wait()
    load_values.wait()

    @pl.loop(0, kv_heads)
    def _(head):
        for one in load_head(head):
            one.wait()
        column = span(head, HD)
        for at in range(BLOCKS - 1, -1, -1):
            reach = (at + 1) * rows
            at_rows = slice(at * rows, reach)
            for part in range(groups // together):
                columns = slice(part * lanes, (part + 1) * lanes)
                grad_h = stacked(grad, at_rows, head * groups + part * together, together)
                grad_probs = times(values[:reach, column], grad_h, ((1,), (1,)))
                probs_low = probs[at][head, :, columns].astype(WIDE)
                delta = jnp.sum(probs_low * grad_probs, axis=0, keepdims=True)
                scaled_low = (probs_low * (grad_probs - delta) * SCALING).astype(LOW)
                scores[:reach, columns] = scaled_low
            turned = times(scores[:reach, :], key[:reach, column], ((0,), (0,))).astype(LOW)
            for one in range(groups):
                grad_query[at_rows, span(head * groups + one, HD)] = turned[
                    one * rows : (one + 1) * rows, :
                ]
            query_h = stacked(query, at_rows, head * groups, groups)
            term = times(scores[:reach, :], query_h)
            if at == BLOCKS - 1:
                total[:reach, :] = term
            else:
                total[:reach, :] += term
        grad_key[:, column] = total[...].astype(LOW)
        store_head(head).start()

    store_key = copy(grad_key, grad_key_hbm, out_sem.at[1])
    store_key.start()
    store_came.wait()
    store_key.wait()
    for at in range(tiles):
        store_weight(at).wait()
    for head in range(kv_heads):
        store_head(head).wait()


def late_call(inputs, grad_all, came, query, grad, key, values, probs):
    length, width = query.shape
    columns = grad_all.shape[1]
    kv_heads = key.shape[1] // HD
    groups = width // key.shape[1]
    rows = length // BLOCKS
    tile = math.gcd(width, 2048)
    tiles = width // tile
    any_spec = pl.BlockSpec(memory_space=pl.ANY)
    dma = pltpu.SemaphoreType.DMA
    shape = jax.ShapeDtypeStruct
    scratch = [pltpu.VMEM(one.shape, LOW) for one in probs]
    scratch += [
        pltpu.VMEM(one.shape, LOW) for one in (inputs, grad_all, came, query, grad, key, values)
    ]
    scratch += [
        pltpu.VMEM((width, columns), LOW),
        pltpu.VMEM(query.shape, LOW),
        pltpu.VMEM(key.shape, LOW),
        pltpu.VMEM((length, HD), WIDE),
        pltpu.VMEM((length, groups * rows), LOW),
        dma((4,)),
        dma((tiles,)),
        dma((tiles,)),
        dma((kv_heads,)),
        dma((kv_heads,)),
        dma((BLOCKS, kv_heads)),
        dma((kv_heads,)),
        dma((2,)),
    ]
    pairs = kv_heads * groups * length * length
    return pl.pallas_call(
        functools.partial(late_kernel, groups, tile),
        in_specs=[any_spec] * (7 + BLOCKS),
        out_specs=[any_spec] * 4,
        out_shape=[
            shape((width, columns), LOW),
            shape(query.shape, LOW),
            shape(key.shape, LOW),
            shape(query.shape, LOW),
        ],
        scratch_shapes=scratch,
        compiler_params=pltpu.CompilerParams(vmem_limit_bytes=60 * 2**20),
        cost_estimate=pl.CostEstimate(
            flops=pairs * HD * 6 + 2 * length * width * columns,
            bytes_accessed=12 * query.size + 2 * width * columns,
            transcendentals=0,
        ),
        name="weight_query_key_grads",
    )(inputs, grad_all, came, query, grad, key, values, *probs)


def join_kernel(arrived_ref, joined_in, joined_hbm, sem):
    copy = pltpu.make_async_copy(arrived_ref, joined_hbm.at[: arrived_ref.shape[0]], sem)
    copy.start()
    copy.wait()


def join_call(arrived, joined):
    any_spec = pl.BlockSpec(memory_space=pl.ANY)
    return pl.pallas_call(
        join_kernel,
        in_specs=[any_spec, any_spec],
        out_specs=any_spec,
        out_shape=jax.ShapeDtypeStruct(joined.shape, joined.dtype),
        input_output_aliases={1: 0},
        scratch_shapes=[pltpu.SemaphoreType.DMA],
        compiler_params=pltpu.CompilerParams(vmem_limit_bytes=2**20),
        name="join_rows",
    )(arrived, joined)


def shards(pipes, ranks, tokens_x, queries, key_rows, out_grad, value_weight, doc_starts):
    inputs = tokens_x[0]
    query, key, grad = queries[0], key_rows[0], out_grad[0]
    came, rest, grad_all, values, *probs = early_call(
        pipes, ranks, doc_starts, query, grad, key, value_weight[0], inputs
    )
    pairs = [(source, source - 1) for source in range(1, pipes)]
    arrived = lax.ppermute(rest, "pipe", pairs)
    weight_grad, grad_query, grad_key, joined = late_call(
        inputs, grad_all, came, query, grad, key, values, probs
    )
    joined = join_call(arrived, joined)
    return (grad_query[None], grad_key[None], weight_grad[None], joined[None])


def solution(mesh):
    pipes, ranks = mesh.shape["pipe"], mesh.shape["tensor"]
    wide, panel = P("pipe", None, "tensor"), P("pipe", "tensor", None)
    return jax.shard_map(
        functools.partial(shards, pipes, ranks),
        mesh=mesh,
        in_specs=(wide, wide, wide, wide, panel, P("pipe", None)),
        out_specs=(wide, wide, panel, wide),
        check_vma=False,
    )
```
